256 devices in a mesh: segment: 4 (over y_hi, core), expert: 64 (over z, x, y_lo).
Axes of the slice: x: 4, y: 4 (y_hi: 2, y_lo: 2; y = y_hi * 2 + y_lo), z: 8, core: 2. Of those that a mesh axis runs over, the one named last changes fastest.
Arguments:
- fwd_tokens: bfloat16 [16384, 2048], P(('segment', 'expert')), may hold values from -6 to 6
- fwd_routes: int32 [16384, 8], P(('segment', 'expert')), may hold values from 0 to 63, all different within a row; in each aligned block of 64 rows (0 to 63, 64 to 127, ...) at most 9 rows name the same one
- fwd_gates: int32 [16384, 8], P(('segment', 'expert')), may hold values from 16 to 255
- bwd_tokens: bfloat16 [16384, 2048], P(('segment', 'expert')), may hold values from -6 to 6
- bwd_routes: int32 [16384, 8], P(('segment', 'expert')), may hold values from 0 to 63, all different within a row; in each aligned block of 64 rows (0 to 63, 64 to 127, ...) at most 9 rows name the same one
- bwd_gates: int32 [16384, 8], P(('segment', 'expert')), may hold values from 16 to 255
- bwd_cotangent: bfloat16 [16384, 2048], P(('segment', 'expert')), may hold values from -6 to 6
- norm_gain: float32 [4, 2048], P('segment'), may hold values from 0.1 to 1.9
- weight_in: bfloat16 [4, 64, 2048, 1536], P('segment', 'expert'), may hold values from -0.125 to 0.125
- weight_out: bfloat16 [4, 64, 768, 2048], P('segment', 'expert'), may hold values from -0.21875 to 0.21875
Outputs:
- passed_forward: bfloat16 [16384, 2048], P(('segment', 'expert'))
- passed_backward: bfloat16 [16384, 2048], P(('segment', 'expert'))
The draws below stay inside these ranges and needn't reach their ends.
Inputs may be any that keep to these rules, and one draw needn't show every extreme that they name: `fwd_routes`: each row names 8 different experts. Among the 64 rows of one device no expert is named more than 9 times, and in every draw some expert is named exactly 9 times by one device's rows. `bwd_routes`: as for fwd_routes.
All inputs are finite; a program needn't handle non-finite values.
Results may differ from the reference program's by a relative error of at most 0.0063.
Values may be sent and summed in bfloat16 or wider, within the bound.
No kernel may reach another device: no remote copies, remote signals or barrier semaphores. Data moves between devices by JAX's collectives and lax.ppermute only.
A program may use at most 128 MiB of HBM per device.

```python
import math
import jax
import jax.numpy as jnp
import numpy as np
from jax import lax

D = 2048
FF = 768
TOP = 8
TOK_DEV = 64
EXPERTS = 64
MOST = 9
TOKENS = 16384
N_SEGMENT = 4
N_EXPERT = 64


def plant(drawn, stream_key, low, high):
    dims = drawn.shape
    spot = [jax.random.randint(jax.random.fold_in(stream_key, axis), (), 0, dims[axis]) for axis in range(len(dims))]
    drawn = drawn.at[tuple(spot)].set(low)
    longest = dims.index(max(dims))
    spot[longest] = (spot[longest] + 1) % dims[longest]
    return drawn.at[tuple(spot)].set(high)


def level_of(key, extent, cuts, smallest, top_value):
    loudness, own = 1.0, jax.random.fold_in(key, 6)
    for position, parts in cuts:
        heights = jnp.exp(jax.random.uniform(jax.random.fold_in(own, position), (parts,), jnp.float32, smallest / len(cuts), top_value / len(cuts)))
        loudness = loudness * jnp.repeat(heights, extent[position] // parts).reshape([-1 if axis == position else 1 for axis in range(len(extent))])
    return loudness


def routed_block(key, own, number, rows, number_of, top, bound, skew):
    sequence = jax.random.permutation(key, number_of)
    packed, common = load_shares(number_of, rows * top, bound, skew, True), load_shares(number_of, rows * top, bound, skew, False)
    places = jnp.arange(number_of)

    def named(lengths, offset_by):
        used = int((lengths > 0).sum())
        fixed = max(1, used // 4)
        shifted = fixed + (places - fixed + offset_by * (used - fixed)) % max(1, number_of - fixed)
        return jnp.zeros((number_of,), jnp.int32).at[sequence[jnp.where(places < fixed, places, shifted)]].set(jnp.asarray(lengths, jnp.int32))

    lengths = jnp.where(number % 4 == 0, named(packed, number // 4), named(common, number - number // 4 - 1))
    mixed = jax.random.permutation(jax.random.fold_in(own, 3), number_of)
    donor, sink = mixed[0:number_of // 2 * 2:2], mixed[1:number_of // 2 * 2:2]
    slack = jnp.minimum(lengths[donor] - 1, bound - lengths[sink]) // 2
    slack = jnp.where((donor == sequence[0]) | (sink == sequence[0]) | (lengths[sink] == 0), 0, jnp.maximum(slack, 0))
    shifted = jax.random.randint(jax.random.fold_in(own, 4), (number_of // 2,), 0, 1 << 20) % (slack + 1)
    lengths = lengths.at[donor].add(-shifted).at[sink].add(shifted)
    labels = jnp.searchsorted(jnp.cumsum(lengths), jnp.arange(rows * top), side="right").astype(jnp.int32)
    listing = labels.reshape(top, rows).T
    listing = listing[jax.random.permutation(jax.random.fold_in(own, 1), rows)]
    offset_by = jax.random.randint(jax.random.fold_in(own, 2), (rows, 1), 0, top)
    return jnp.take_along_axis(listing, (jnp.arange(top)[None, :] + offset_by) % top, axis=1)


def load_shares(amount, total, limit, lean, full):
    weights = [(1 << 20) // math.isqrt(standing ** lean) + 1 for standing in range(1, amount + 1)]
    largest = limit if full else min(limit, max(-(-total // amount), total * weights[0] // sum(weights)))
    least = 1 if total - largest >= amount - 1 else 0
    counts, spare = [largest] + [least] * (amount - 1), total - largest - least * (amount - 1)
    while spare > 0:
        movable = [i for i in range(1, amount) if counts[i] < largest] or [i for i in range(1, amount) if counts[i] < limit]
        mass, budget = sum([weights[i] for i in movable]), spare
        for i in movable:
            more = min(limit - counts[i], max(1, budget * weights[i] // mass), spare)
            counts[i] = counts[i] + more
            spare = spare - more
    return np.array(counts)


def scatter_about(own_key, extent, scale, bound, split=(), held_as=jnp.bfloat16):
    level = level_of(own_key, extent, split, -0.22, 0.18) if split else 1.0
    values = jax.random.normal(own_key, extent, jnp.float32) * scale * level
    return jnp.minimum(jnp.maximum(values, -bound), bound).astype(held_as)


def setup_inputs(seed: int = 0) -> dict:
    keys = jax.random.split(jax.random.key(seed), 11)
    fwd_tokens = scatter_about(keys[0], (TOKENS, D), 1.0, 6.0, ((0, 256),))
    fwd_routes_keys = jax.random.split(jax.random.fold_in(keys[1], 1), TOKENS // TOK_DEV)
    fwd_routes_turns = jax.random.permutation(jax.random.fold_in(keys[1], 3), TOKENS // TOK_DEV)
    fwd_routes = jax.vmap(lambda own, number: routed_block(jax.random.fold_in(keys[1], 2), own, number, TOK_DEV, EXPERTS, TOP, MOST, 2))(fwd_routes_keys, fwd_routes_turns).reshape((TOKENS, TOP))
    fwd_gates = plant(jax.random.randint(keys[2], (TOKENS, TOP), 16, 256), jax.random.fold_in(keys[2], 1), 16, 255).astype(jnp.int32)
    bwd_tokens = scatter_about(keys[3], (TOKENS, D), 1.0, 6.0, ((0, 256),))
    bwd_routes_keys = jax.random.split(jax.random.fold_in(keys[4], 1), TOKENS // TOK_DEV)
    bwd_routes_turns = jax.random.permutation(jax.random.fold_in(keys[4], 3), TOKENS // TOK_DEV)
    bwd_routes = jax.vmap(lambda own, number: routed_block(jax.random.fold_in(keys[4], 2), own, number, TOK_DEV, EXPERTS, TOP, MOST, 2))(bwd_routes_keys, bwd_routes_turns).reshape((TOKENS, TOP))
    bwd_gates = plant(jax.random.randint(keys[5], (TOKENS, TOP), 16, 256), jax.random.fold_in(keys[5], 1), 16, 255).astype(jnp.int32)
    bwd_cotangent = scatter_about(keys[6], (TOKENS, D), 1.0, 6.0, ((0, 256),))
    norm_gain = jnp.clip(1.0 + 0.18 * jax.random.normal(keys[7], (N_SEGMENT, D), jnp.float32), 0.1, 1.9)
    weight_in = scatter_about(keys[8], (N_SEGMENT, EXPERTS, D, 2 * FF), D ** -0.5, 0.125, ((0, 4), (1, 64)))
    weight_out = scatter_about(keys[9], (N_SEGMENT, EXPERTS, FF, D), FF ** -0.5, 0.21875, ((0, 4), (1, 64)))
    return dict(fwd_tokens=fwd_tokens, fwd_routes=fwd_routes, fwd_gates=fwd_gates, bwd_tokens=bwd_tokens, bwd_routes=bwd_routes, bwd_gates=bwd_gates, bwd_cotangent=bwd_cotangent, norm_gain=norm_gain, weight_in=weight_in, weight_out=weight_out)


eps = 1e-06

def rms_scale(values):
    return lax.rsqrt(lax.optimization_barrier(jnp.mean(values * values, axis=-1, keepdims=True)) + eps)

def expert_forward(in_rows, w_first, w_second):
    gate_up = jnp.dot(in_rows, w_first, preferred_element_type=jnp.float32)
    hidden_width = w_second.shape[0]
    hidden = (jax.nn.silu(gate_up[:, :hidden_width]) * gate_up[:, hidden_width:]).astype(jnp.bfloat16)
    return jnp.dot(hidden, w_second, preferred_element_type=jnp.float32).astype(jnp.bfloat16)

def expert_backward(in_rows, out_grad, w_first, w_second):
    gate_up = jnp.dot(in_rows, w_first, preferred_element_type=jnp.float32)
    hidden_width = w_second.shape[0]
    gate_part = gate_up[:, :hidden_width]
    up_part = gate_up[:, hidden_width:]
    sigmoid_gate = jax.nn.sigmoid(gate_part)
    activated = gate_part * sigmoid_gate
    slope = sigmoid_gate * (1.0 + gate_part * (1.0 - sigmoid_gate))
    hidden_grad = lax.dot_general(out_grad, w_second, (((1,), (1,)), ((), ())), preferred_element_type=jnp.float32)
    pre_grad = jnp.concatenate([hidden_grad * up_part * slope, hidden_grad * activated], axis=1).astype(jnp.bfloat16)
    return lax.dot_general(pre_grad, w_first, (((1,), (1,)), ((), ())), preferred_element_type=jnp.float32).astype(jnp.bfloat16)

def route_sum(in_rows, grad_rows, routes, gate_codes, w_first_all, w_second_all, with_grad):
    flat_routes = routes.reshape(-1).astype(jnp.int32)
    row_total = flat_routes.shape[0]
    tok_rows = in_rows.shape[0]
    width = in_rows.shape[1]
    padded_in = jnp.concatenate([in_rows, jnp.zeros((1, width), in_rows.dtype)], axis=0)
    padded_grad = jnp.concatenate([grad_rows, jnp.zeros((1, width), grad_rows.dtype)], axis=0)
    gate_flat = jnp.concatenate([gate_codes.reshape(-1).astype(jnp.float32) / 256.0, jnp.zeros((1,), jnp.float32)])
    slots = N_EXPERT * MOST

    def one_expert(total, items):
        expert_id, w_first, w_second = items
        picked = jnp.nonzero(flat_routes == expert_id, size=slots, fill_value=row_total)[0].astype(jnp.int32)
        token_ids = jnp.where(picked < row_total, picked // TOP, tok_rows).astype(jnp.int32)
        if with_grad:
            result = expert_backward(padded_in[token_ids], padded_grad[token_ids], w_first, w_second)
        else:
            result = expert_forward(padded_in[token_ids], w_first, w_second)
        contrib = gate_flat[picked][:, None] * result.astype(jnp.float32)
        return (total.at[token_ids].add(contrib), None)
    start = jnp.zeros((tok_rows + 1, width), jnp.float32)
    expert_ids = jnp.arange(EXPERTS, dtype=jnp.int32)
    total, _ = lax.scan(one_expert, start, (expert_ids, w_first_all, w_second_all))
    return total[:tok_rows]

def reference(fwd_tokens, fwd_routes, fwd_gates, bwd_tokens, bwd_routes, bwd_gates, bwd_cotangent, norm_gain, weight_in, weight_out):
    segment_rows = N_EXPERT * TOK_DEV
    forward_list = []
    backward_list = []
    for section in range(N_SEGMENT):
        lower = section * segment_rows
        upper = lower + segment_rows
        gain = norm_gain[section]
        fwd32 = fwd_tokens[lower:upper].astype(jnp.float32)
        fwd_normed = (fwd32 * rms_scale(fwd32) * gain).astype(jnp.bfloat16)
        fwd_moe = route_sum(fwd_normed, fwd_tokens[lower:upper], fwd_routes[lower:upper], fwd_gates[lower:upper], weight_in[section], weight_out[section], False)
        forward_list.append((fwd32 + fwd_moe).astype(jnp.bfloat16))
        bwd32 = bwd_tokens[lower:upper].astype(jnp.float32)
        bwd_scale = rms_scale(bwd32)
        bwd_base = bwd32 * bwd_scale
        bwd_normed = (bwd_base * gain).astype(jnp.bfloat16)
        cotangent = bwd_cotangent[lower:upper]
        norm_grad = route_sum(bwd_normed, cotangent, bwd_routes[lower:upper], bwd_gates[lower:upper], weight_in[section], weight_out[section], True)
        scaled = norm_grad * gain
        input_grad = cotangent.astype(jnp.float32) + bwd_scale * (scaled - bwd_base * lax.optimization_barrier(jnp.mean(scaled * bwd_base, axis=-1, keepdims=True)))
        backward_list.append(input_grad.astype(jnp.bfloat16))
    forward_all = jnp.stack(forward_list)
    backward_all = jnp.stack(backward_list)
    passed_forward = jnp.roll(forward_all, 1, axis=0).reshape(-1, D)
    passed_backward = jnp.roll(backward_all, -1, axis=0).reshape(-1, D)
    return (passed_forward, passed_backward)
```

```python
import jax
import jax.numpy as jnp
from jax import lax
from jax.experimental import pallas as pl
from jax.experimental.pallas import tpu as pltpu
from jax.sharding import Mesh, PartitionSpec as P

eps = 1e-06
most = 9
bf16 = jnp.bfloat16
f32 = jnp.float32


def rms_scale(values):
    return lax.rsqrt(jnp.mean(values * values, axis=-1, keepdims=True) + eps)


def shifted(value, axis, steps):
    count = lax.axis_size(axis)
    return lax.ppermute(value, axis, [(s, (s + steps) % count) for s in range(count)])


def gather_ring(value, axis):
    count = lax.axis_size(axis)
    found = {0: value}
    up = down = value
    for k in range(1, count // 2 + 1):
        up = shifted(up, axis, 1)
        found[k] = up
        if k < count - count // 2:
            down = shifted(down, axis, -1)
            found[count - k] = down
    return [found[j] for j in range(count)]


def reduce_ring(weigh, rows, axis):
    count = lax.axis_size(axis)
    far = count // 2
    tokens = weigh.shape[0] // count
    part = {}
    for low, high in ((far, far + 2), (0, far), (far + 2, count)):
        total = jnp.dot(
            weigh[low * tokens : high * tokens], rows, preferred_element_type=f32
        )
        for j in range(low, high):
            part[j] = total[(j - low) * tokens : (j - low + 1) * tokens]
    down = up = None
    for k in range(far, 0, -1):
        give = part[k] if down is None else part[k] + down.astype(f32)
        give = give.astype(bf16)
        down = shifted(give, axis, -1)
        if k <= count - 1 - far:
            give = part[count - k] if up is None else part[count - k] + up.astype(f32)
            give = give.astype(bf16)
            up = shifted(give, axis, 1)
    return part[0] + down.astype(f32) + up.astype(f32)


def plane_exchange(rows, axes, blocks):
    width = rows.shape[-1]
    out = lax.all_to_all(rows.reshape(blocks, -1, width), axes, 0, 0, tiled=True)
    return out.reshape(-1, width)


def first_rows(tokens, gain, tables):
    rows, width = tokens.shape
    top = tables[0].shape[0]

    def kernel(tok_ref, gain_ref, *refs):
        out_ref = refs[-1]
        x = tok_ref[...].astype(f32)
        scale = lax.rsqrt(jnp.mean(x * x, axis=-1, keepdims=True) + eps)
        out_ref[:, :width] = (x * scale * gain_ref[...]).astype(bf16)
        total = jnp.zeros((rows, 128), f32)
        for i in range(4):
            ids = lax.broadcasted_iota(jnp.int32, (top, 128), 0) + i * top
            lanes = lax.broadcasted_iota(jnp.int32, (top, 128), 1)
            move = jnp.where(ids == lanes, 1.0, 0.0).astype(bf16)
            codes = refs[i][...].astype(f32).astype(bf16)
            total = total + lax.dot_general(
                codes, move, (((0,), (0,)), ((), ())), preferred_element_type=f32
            )
        out_ref[:, width:] = total.astype(bf16)

    return pl.pallas_call(
        kernel, out_shape=jax.ShapeDtypeStruct((rows, width + 128), bf16), name="first_rows"
    )(tokens, gain, *tables)


def routed_send(blocks, tabled, lane, top, plane, first, width):
    count = len(blocks)
    rows = blocks[0].shape[0]
    slots = most * count
    total = plane * slots
    step = min(1024, width)

    def kernel(first_ref, *refs):
        tab = refs[:count]
        src = refs[count : 2 * count]
        send_ref, place_ref, weigh_ref = refs[2 * count :]

        @pl.when(pl.program_id(0) == 0)
        def _():
            table = jnp.concatenate([r[...] for r in tab], axis=0).astype(f32)
            lanes = lax.broadcasted_iota(jnp.int32, (count * rows, 128), 1)
            wanted = jnp.where(lanes < plane, lanes + first_ref[0], -5).astype(f32)
            named = jnp.zeros((count * rows, 128), f32)
            gates = jnp.zeros((count * rows, 128), f32)
            for k in range(top):
                same = table[:, lane + k : lane + k + 1] == wanted
                named = named + jnp.where(same, 1.0, 0.0)
                gates = gates + jnp.where(same, table[:, lane + top + k : lane + top + k + 1], 0.0)
            r0 = lax.broadcasted_iota(jnp.int32, (rows, rows), 0)
            r1 = lax.broadcasted_iota(jnp.int32, (rows, rows), 1)
            earlier = jnp.where(r1 < r0, 1.0, 0.0).astype(bf16)
            ranks = [
                jnp.dot(
                    earlier,
                    named[j * rows : (j + 1) * rows].astype(bf16),
                    preferred_element_type=f32,
                )
                + float(j * most)
                for j in range(count)
            ]
            code = jnp.where(named > 0.5, jnp.concatenate(ranks, axis=0), -1.0)
            flipped = code.T
            ids = lax.broadcasted_iota(jnp.int32, (slots, count * rows), 0).astype(f32)
            placed = [
                jnp.where(flipped[p : p + 1, :] == ids, 1.0, 0.0) for p in range(plane)
            ]
            place_ref[...] = jnp.concatenate(placed, axis=0).astype(bf16)
            p0 = lax.broadcasted_iota(jnp.int32, (128, total), 0) * slots
            n0 = lax.broadcasted_iota(jnp.int32, (128, total), 1)
            spread = jnp.where((n0 >= p0) & (n0 < p0 + slots), 1.0, 0.0).astype(bf16)
            n1 = lax.broadcasted_iota(jnp.int32, (8, total), 1)
            slot_of = n1
            for p in range(1, plane):
                slot_of = slot_of - jnp.where(n1 >= p * slots, slots, 0)
            slot_of = slot_of.astype(f32)[0:1]
            wide_code = jnp.dot(code.astype(bf16), spread, preferred_element_type=f32)
            wide_gate = jnp.dot(
                (gates * (1.0 / 256.0)).astype(bf16), spread, preferred_element_type=f32
            )
            weigh_ref[...] = jnp.where(wide_code == slot_of, wide_gate, 0.0).astype(bf16)

        gathered = jnp.concatenate([r[...] for r in src], axis=0)
        send_ref[...] = jnp.dot(
            place_ref[...], gathered, preferred_element_type=f32
        ).astype(bf16)

    at = tabled[0].shape[1] // 128 - 1
    return pl.pallas_call(
        kernel,
        grid=(width // step,),
        in_specs=[pl.BlockSpec(memory_space=pltpu.SMEM)]
        + [pl.BlockSpec((rows, 128), lambda c: (0, at))] * count
        + [pl.BlockSpec((rows, step), lambda c: (0, c))] * count,
        out_specs=[
            pl.BlockSpec((total, step), lambda c: (0, c)),
            pl.BlockSpec((total, count * rows), lambda c: (0, 0)),
            pl.BlockSpec((count * rows, total), lambda c: (0, 0)),
        ],
        out_shape=[
            jax.ShapeDtypeStruct((total, width), bf16),
            jax.ShapeDtypeStruct((total, count * rows), bf16),
            jax.ShapeDtypeStruct((count * rows, total), bf16),
        ],
        name="routed_send",
    )(first, *tabled, *blocks)


def placed_send(blocks, place, width):
    count = len(blocks)
    rows = blocks[0].shape[0]
    total = place.shape[0]
    step = min(1024, width)

    def kernel(place_ref, *refs):
        gathered = jnp.concatenate([r[...] for r in refs[:count]], axis=0)
        refs[count][...] = jnp.dot(
            place_ref[...], gathered, preferred_element_type=f32
        ).astype(bf16)

    return pl.pallas_call(
        kernel,
        grid=(width // step,),
        in_specs=[pl.BlockSpec((total, count * rows), lambda c: (0, 0))]
        + [pl.BlockSpec((rows, step), lambda c: (0, c))] * count,
        out_specs=pl.BlockSpec((total, step), lambda c: (0, c)),
        out_shape=jax.ShapeDtypeStruct((total, width), bf16),
        name="placed_send",
    )(place, *blocks)


def expert_forward(in_rows, w_first, w_second):
    gate_up = jnp.dot(in_rows, w_first, preferred_element_type=f32)
    hidden_width = w_second.shape[0]
    hidden = (jax.nn.silu(gate_up[:, :hidden_width]) * gate_up[:, hidden_width:]).astype(bf16)
    return jnp.dot(hidden, w_second, preferred_element_type=f32).astype(bf16)


def expert_backward(in_rows, out_grad, w_first, w_second):
    gate_up = jnp.dot(in_rows, w_first, preferred_element_type=f32)
    hidden_width = w_second.shape[0]
    gate_part = gate_up[:, :hidden_width]
    up_part = gate_up[:, hidden_width:]
    sigmoid_gate = jax.nn.sigmoid(gate_part)
    activated = gate_part * sigmoid_gate
    slope = sigmoid_gate * (1.0 + gate_part * (1.0 - sigmoid_gate))
    hidden_grad = lax.dot_general(
        out_grad, w_second, (((1,), (1,)), ((), ())), preferred_element_type=f32
    )
    pre_grad = jnp.concatenate(
        [hidden_grad * up_part * slope, hidden_grad * activated], axis=1
    ).astype(bf16)
    return lax.dot_general(
        pre_grad, w_first, (((1,), (1,)), ((), ())), preferred_element_type=f32
    ).astype(bf16)


def inner(
    fwd_tokens,
    fwd_routes,
    fwd_gates,
    bwd_tokens,
    bwd_routes,
    bwd_gates,
    bwd_cotangent,
    norm_gain,
    weight_in,
    weight_out,
):
    plane = lax.axis_size("x") * lax.axis_size("y")
    _, top = fwd_routes.shape
    width = fwd_tokens.shape[1]
    w_first = weight_in[0, 0]
    w_second = weight_out[0, 0]
    gain = norm_gain[0]
    fwd32 = fwd_tokens.astype(f32)
    bwd32 = bwd_tokens.astype(f32)
    bwd_scale = rms_scale(bwd32)
    bwd_base = bwd32 * bwd_scale
    bwd_normed = (bwd_base * gain).astype(bf16)

    first = (lax.axis_index("z") * plane).astype(jnp.int32).reshape(1)
    tables = tuple(t.T for t in (fwd_routes, fwd_gates, bwd_routes, bwd_gates))
    fwd_blocks = gather_ring(first_rows(fwd_tokens, norm_gain, tables), "z")
    bwd_blocks = gather_ring(bwd_normed, "z")
    grad_blocks = gather_ring(bwd_cotangent, "z")

    fwd_send, _, fwd_weigh = routed_send(
        fwd_blocks, fwd_blocks, 0, top, plane, first, width
    )
    fwd_rows = plane_exchange(fwd_send, ("x", "y"), plane)
    bwd_send, bwd_place, bwd_weigh = routed_send(
        bwd_blocks, fwd_blocks, 2 * top, top, plane, first, width
    )
    bwd_rows = plane_exchange(bwd_send, ("x", "y"), plane)
    grad_send = placed_send(grad_blocks, bwd_place, width)
    grad_rows = plane_exchange(grad_send, ("x", "y"), plane)

    fwd_result = expert_forward(fwd_rows, w_first, w_second)
    fwd_back = plane_exchange(fwd_result, ("x", "y"), plane)
    bwd_result = expert_backward(bwd_rows, grad_rows, w_first, w_second)
    bwd_back = plane_exchange(bwd_result, ("x", "y"), plane)

    fwd_moe = reduce_ring(fwd_weigh, fwd_back, "z")
    layer_out = (fwd32 + fwd_moe).astype(bf16)
    passed_forward = shifted(layer_out, "segment", 1)
    norm_grad = reduce_ring(bwd_weigh, bwd_back, "z")
    scaled = norm_grad * gain
    input_grad = bwd_cotangent.astype(f32) + bwd_scale * (
        scaled - bwd_base * jnp.mean(scaled * bwd_base, axis=-1, keepdims=True)
    )
    passed_backward = shifted(input_grad.astype(bf16), "segment", -1)
    return (passed_forward, passed_backward)


def solution(mesh):
    cut = Mesh(mesh.devices.reshape(4, 8, 4, 2), ("segment", "z", "x", "y"))
    rows = P(("segment", "z", "x", "y"), None)
    placed = (rows,) * 7 + (
        P("segment", None),
        P("segment", ("z", "x", "y"), None, None),
        P("segment", ("z", "x", "y"), None, None),
    )
    return jax.shard_map(inner, mesh=cut, in_specs=placed, out_specs=(rows, rows), check_vma=False)
```

```python
import jax
import jax.numpy as jnp
from jax import lax
from jax.experimental import pallas as pl
from jax.experimental.pallas import tpu as pltpu
from jax.sharding import Mesh, PartitionSpec as P

eps = 1e-06
most = 9
bf16 = jnp.bfloat16
f32 = jnp.float32


def rms_scale(values):
    return lax.rsqrt(jnp.mean(values * values, axis=-1, keepdims=True) + eps)


def shifted(value, axis, steps):
    count = lax.axis_size(axis)
    return lax.ppermute(value, axis, [(s, (s + steps) % count) for s in range(count)])


def gather_ring(value, axis):
    count = lax.axis_size(axis)
    found = {0: value}
    up = down = value
    for k in range(1, count // 2 + 1):
        up = shifted(up, axis, 1)
        found[k] = up
        if k < count - count // 2:
            down = shifted(down, axis, -1)
            found[count - k] = down
    return [found[j] for j in range(count)]


order = (1, 5, 3, 7, 2, 6, 0, 4)


def passed(value, sections, planes):
    held, count = lax.axis_size("segment"), lax.axis_size("z")
    pairs = [
        (s * count + z, ((s + sections) % held) * count + (z + planes) % count)
        for s in range(held)
        for z in range(count)
    ]
    return lax.ppermute(value, ("segment", "z"), pairs)


def reduce_hops(weigh, rows, sections):
    tokens = weigh.shape[0] // len(order)

    def some(low, high):
        return jnp.dot(
            weigh[low * tokens : high * tokens], rows, preferred_element_type=f32
        )

    up = some(0, 2).astype(bf16)
    up = shifted(up, "z", 1)
    down = some(2, 4).astype(bf16)
    down = shifted(down, "z", -1)
    stay = some(4, 6)
    own = some(6, 7).astype(bf16)
    own = passed(own, sections, 0)
    far = some(7, 8).astype(bf16)
    far = passed(far, sections, 4)
    back = (stay[:tokens] + up[:tokens].astype(f32) + down[:tokens].astype(f32)).astype(bf16)
    back = passed(back, sections, -2)
    ahead = (stay[tokens:] + up[tokens:].astype(f32) + down[tokens:].astype(f32)).astype(bf16)
    ahead = passed(ahead, sections, 2)
    return own.astype(f32) + far.astype(f32) + back.astype(f32) + ahead.astype(f32)


def plane_exchange(rows, axes, blocks):
    width = rows.shape[-1]
    out = lax.all_to_all(rows.reshape(blocks, -1, width), axes, 0, 0, tiled=True)
    return out.reshape(-1, width)


def first_rows(tokens, gain, tables):
    rows, width = tokens.shape
    top = tables[0].shape[0]

    def kernel(tok_ref, gain_ref, *refs):
        out_ref = refs[-1]
        x = tok_ref[...].astype(f32)
        scale = lax.rsqrt(jnp.mean(x * x, axis=-1, keepdims=True) + eps)
        out_ref[:, :width] = (x * scale * gain_ref[...]).astype(bf16)
        total = jnp.zeros((rows, 128), f32)
        for i in range(4):
            ids = lax.broadcasted_iota(jnp.int32, (top, 128), 0) + i * top
            lanes = lax.broadcasted_iota(jnp.int32, (top, 128), 1)
            move = jnp.where(ids == lanes, 1.0, 0.0).astype(bf16)
            codes = refs[i][...].astype(f32).astype(bf16)
            total = total + lax.dot_general(
                codes, move, (((0,), (0,)), ((), ())), preferred_element_type=f32
            )
        out_ref[:, width:] = total.astype(bf16)

    return pl.pallas_call(
        kernel, out_shape=jax.ShapeDtypeStruct((rows, width + 128), bf16), name="first_rows"
    )(tokens, gain, *tables)


def routed_send(blocks, tabled, lane, top, plane, first, width):
    count = len(blocks)
    rows = blocks[0].shape[0]
    slots = most * count
    total = plane * slots
    step = min(1024, width)

    def kernel(first_ref, *refs):
        tab = refs[:count]
        src = refs[count : 2 * count]
        send_ref, place_ref, weigh_ref = refs[2 * count :]

        @pl.when(pl.program_id(0) == 0)
        def _():
            table = jnp.concatenate([r[...] for r in tab], axis=0).astype(f32)
            lanes = lax.broadcasted_iota(jnp.int32, (count * rows, 128), 1)
            wanted = jnp.where(lanes < plane, lanes + first_ref[0], -5).astype(f32)
            named = jnp.zeros((count * rows, 128), f32)
            gates = jnp.zeros((count * rows, 128), f32)
            for k in range(top):
                same = table[:, lane + k : lane + k + 1] == wanted
                named = named + jnp.where(same, 1.0, 0.0)
                gates = gates + jnp.where(same, table[:, lane + top + k : lane + top + k + 1], 0.0)
            r0 = lax.broadcasted_iota(jnp.int32, (rows, rows), 0)
            r1 = lax.broadcasted_iota(jnp.int32, (rows, rows), 1)
            earlier = jnp.where(r1 < r0, 1.0, 0.0).astype(bf16)
            ranks = [
                jnp.dot(
                    earlier,
                    named[j * rows : (j + 1) * rows].astype(bf16),
                    preferred_element_type=f32,
                )
                + float(j * most)
                for j in range(count)
            ]
            code = jnp.where(named > 0.5, jnp.concatenate(ranks, axis=0), -1.0)
            flipped = code.T
            ids = lax.broadcasted_iota(jnp.int32, (slots, count * rows), 0).astype(f32)
            placed = [
                jnp.where(flipped[p : p + 1, :] == ids, 1.0, 0.0) for p in range(plane)
            ]
            place_ref[...] = jnp.concatenate(placed, axis=0).astype(bf16)
            p0 = lax.broadcasted_iota(jnp.int32, (128, total), 0) * slots
            n0 = lax.broadcasted_iota(jnp.int32, (128, total), 1)
            spread = jnp.where((n0 >= p0) & (n0 < p0 + slots), 1.0, 0.0).astype(bf16)
            n1 = lax.broadcasted_iota(jnp.int32, (8, total), 1)
            slot_of = n1
            for p in range(1, plane):
                slot_of = slot_of - jnp.where(n1 >= p * slots, slots, 0)
            slot_of = slot_of.astype(f32)[0:1]
            code = jnp.concatenate([code[j * rows : (j + 1) * rows] for j in order], axis=0)
            gates = jnp.concatenate([gates[j * rows : (j + 1) * rows] for j in order], axis=0)
            wide_code = jnp.dot(code.astype(bf16), spread, preferred_element_type=f32)
            wide_gate = jnp.dot(
                (gates * (1.0 / 256.0)).astype(bf16), spread, preferred_element_type=f32
            )
            weigh_ref[...] = jnp.where(wide_code == slot_of, wide_gate, 0.0).astype(bf16)

        gathered = jnp.concatenate([r[...] for r in src], axis=0)
        send_ref[...] = jnp.dot(
            place_ref[...], gathered, preferred_element_type=f32
        ).astype(bf16)

    at = tabled[0].shape[1] // 128 - 1
    return pl.pallas_call(
        kernel,
        grid=(width // step,),
        in_specs=[pl.BlockSpec(memory_space=pltpu.SMEM)]
        + [pl.BlockSpec((rows, 128), lambda c: (0, at))] * count
        + [pl.BlockSpec((rows, step), lambda c: (0, c))] * count,
        out_specs=[
            pl.BlockSpec((total, step), lambda c: (0, c)),
            pl.BlockSpec((total, count * rows), lambda c: (0, 0)),
            pl.BlockSpec((count * rows, total), lambda c: (0, 0)),
        ],
        out_shape=[
            jax.ShapeDtypeStruct((total, width), bf16),
            jax.ShapeDtypeStruct((total, count * rows), bf16),
            jax.ShapeDtypeStruct((count * rows, total), bf16),
        ],
        name="routed_send",
    )(first, *tabled, *blocks)


def placed_send(blocks, place, width):
    count = len(blocks)
    rows = blocks[0].shape[0]
    total = place.shape[0]
    step = min(1024, width)

    def kernel(place_ref, *refs):
        gathered = jnp.concatenate([r[...] for r in refs[:count]], axis=0)
        refs[count][...] = jnp.dot(
            place_ref[...], gathered, preferred_element_type=f32
        ).astype(bf16)

    return pl.pallas_call(
        kernel,
        grid=(width // step,),
        in_specs=[pl.BlockSpec((total, count * rows), lambda c: (0, 0))]
        + [pl.BlockSpec((rows, step), lambda c: (0, c))] * count,
        out_specs=pl.BlockSpec((total, step), lambda c: (0, c)),
        out_shape=jax.ShapeDtypeStruct((total, width), bf16),
        name="placed_send",
    )(place, *blocks)


def expert_forward(in_rows, w_first, w_second):
    gate_up = jnp.dot(in_rows, w_first, preferred_element_type=f32)
    hidden_width = w_second.shape[0]
    hidden = (jax.nn.silu(gate_up[:, :hidden_width]) * gate_up[:, hidden_width:]).astype(bf16)
    return jnp.dot(hidden, w_second, preferred_element_type=f32).astype(bf16)


def expert_backward(in_rows, out_grad, w_first, w_second):
    gate_up = jnp.dot(in_rows, w_first, preferred_element_type=f32)
    hidden_width = w_second.shape[0]
    gate_part = gate_up[:, :hidden_width]
    up_part = gate_up[:, hidden_width:]
    sigmoid_gate = jax.nn.sigmoid(gate_part)
    activated = gate_part * sigmoid_gate
    slope = sigmoid_gate * (1.0 + gate_part * (1.0 - sigmoid_gate))
    hidden_grad = lax.dot_general(
        out_grad, w_second, (((1,), (1,)), ((), ())), preferred_element_type=f32
    )
    pre_grad = jnp.concatenate(
        [hidden_grad * up_part * slope, hidden_grad * activated], axis=1
    ).astype(bf16)
    return lax.dot_general(
        pre_grad, w_first, (((1,), (1,)), ((), ())), preferred_element_type=f32
    ).astype(bf16)


def inner(
    fwd_tokens,
    fwd_routes,
    fwd_gates,
    bwd_tokens,
    bwd_routes,
    bwd_gates,
    bwd_cotangent,
    norm_gain,
    weight_in,
    weight_out,
):
    plane = lax.axis_size("x") * lax.axis_size("y")
    _, top = fwd_routes.shape
    width = fwd_tokens.shape[1]
    w_first = weight_in[0, 0]
    w_second = weight_out[0, 0]
    gain = norm_gain[0]
    bwd32 = bwd_tokens.astype(f32)
    bwd_scale = rms_scale(bwd32)
    bwd_base = bwd32 * bwd_scale
    bwd_normed = (bwd_base * gain).astype(bf16)

    first = (lax.axis_index("z") * plane).astype(jnp.int32).reshape(1)
    tables = tuple(t.T for t in (fwd_routes, fwd_gates, bwd_routes, bwd_gates))
    fwd_blocks = gather_ring(first_rows(fwd_tokens, norm_gain, tables), "z")
    bwd_blocks = gather_ring(bwd_normed, "z")
    grad_blocks = gather_ring(bwd_cotangent, "z")

    fwd_send, _, fwd_weigh = routed_send(
        fwd_blocks, fwd_blocks, 0, top, plane, first, width
    )
    fwd_rows = plane_exchange(fwd_send, ("x", "y"), plane)
    bwd_send, bwd_place, bwd_weigh = routed_send(
        bwd_blocks, fwd_blocks, 2 * top, top, plane, first, width
    )
    bwd_rows = plane_exchange(bwd_send, ("x", "y"), plane)
    grad_send = placed_send(grad_blocks, bwd_place, width)
    grad_rows = plane_exchange(grad_send, ("x", "y"), plane)

    fwd_result = expert_forward(fwd_rows, w_first, w_second)
    fwd_back = plane_exchange(fwd_result, ("x", "y"), plane)
    bwd_result = expert_backward(bwd_rows, grad_rows, w_first, w_second)
    bwd_back = plane_exchange(bwd_result, ("x", "y"), plane)

    fwd_held = passed(fwd_tokens, 1, 0)
    bwd_held = passed(bwd_tokens, -1, 0)
    cotangent = passed(bwd_cotangent, -1, 0)
    gain_held = passed(norm_gain, -1, 0)
    fwd_moe = reduce_hops(fwd_weigh, fwd_back, 1)
    passed_forward = (fwd_held.astype(f32) + fwd_moe).astype(bf16)
    held32 = bwd_held.astype(f32)
    held_scale = rms_scale(held32)
    held_base = held32 * held_scale
    norm_grad = reduce_hops(bwd_weigh, bwd_back, -1)
    scaled = norm_grad * gain_held
    input_grad = cotangent.astype(f32) + held_scale * (
        scaled - held_base * jnp.mean(scaled * held_base, axis=-1, keepdims=True)
    )
    return (passed_forward, input_grad.astype(bf16))


def solution(mesh):
    cut = Mesh(mesh.devices.reshape(4, 8, 4, 2), ("segment", "z", "x", "y"))
    rows = P(("segment", "z", "x", "y"), None)
    placed = (rows,) * 7 + (
        P("segment", None),
        P("segment", ("z", "x", "y"), None, None),
        P("segment", ("z", "x", "y"), None, None),
    )
    return jax.shard_map(inner, mesh=cut, in_specs=placed, out_specs=(rows, rows), check_vma=False)
```

```python
import jax
import jax.numpy as jnp
from jax import lax
from jax.experimental import pallas as pl
from jax.experimental.pallas import tpu as pltpu
from jax.sharding import Mesh, PartitionSpec as P

eps = 1e-06
most = 9
bf16 = jnp.bfloat16
f32 = jnp.float32


def rms_scale(values):
    return lax.rsqrt(jnp.mean(values * values, axis=-1, keepdims=True) + eps)


def shifted(value, axis, steps):
    count = lax.axis_size(axis)
    return lax.ppermute(value, axis, [(s, (s + steps) % count) for s in range(count)])


def gather_ring(value, axis):
    count = lax.axis_size(axis)
    found = {0: value}
    up = down = value
    for k in range(1, count // 2 + 1):
        up = shifted(up, axis, 1)
        found[k] = up
        if k < count - count // 2:
            down = shifted(down, axis, -1)
            found[count - k] = down
    return [found[j] for j in range(count)]


order = (1, 5, 3, 7, 2, 6, 0, 4)


def weighed_sums(weigh, rows):
    total, width = rows.shape
    tokens = weigh.shape[0] // len(order)
    step = min(512, width)
    heights = ((2, bf16), (2, bf16), (2, f32), (1, f32), (1, bf16))

    def kernel(weigh_ref, rows_ref, *refs):
        sums = jnp.dot(weigh_ref[...], rows_ref[...], preferred_element_type=f32)
        low = 0
        for ref, (height, dtype) in zip(refs, heights):
            ref[...] = sums[low * tokens : (low + height) * tokens].astype(dtype)
            low += height

    return pl.pallas_call(
        kernel,
        grid=(width // step,),
        in_specs=[
            pl.BlockSpec((len(order) * tokens, total), lambda c: (0, 0)),
            pl.BlockSpec((total, step), lambda c: (0, c)),
        ],
        out_specs=[pl.BlockSpec((h * tokens, step), lambda c: (0, c)) for h, _ in heights],
        out_shape=[jax.ShapeDtypeStruct((h * tokens, width), d) for h, d in heights],
        name="weighed_sums",
    )(weigh, rows)


def reduce_hops(weigh, rows):
    tokens = weigh.shape[0] // len(order)
    up, down, stay, own, far = weighed_sums(weigh, rows)
    up = shifted(up, "z", 1)
    down = shifted(down, "z", -1)
    far = shifted(far, "z", 4)
    back = (stay[:tokens] + up[:tokens].astype(f32) + down[:tokens].astype(f32)).astype(bf16)
    back = shifted(back, "z", -2)
    ahead = (stay[tokens:] + up[tokens:].astype(f32) + down[tokens:].astype(f32)).astype(bf16)
    ahead = shifted(ahead, "z", 2)
    return own + far.astype(f32) + back.astype(f32) + ahead.astype(f32)


def plane_exchange(rows, axes, blocks):
    width = rows.shape[-1]
    out = lax.all_to_all(rows.reshape(blocks, -1, width), axes, 0, 0, tiled=True)
    return out.reshape(-1, width)


def first_rows(tokens, gain, tables):
    rows, width = tokens.shape
    top = tables[0].shape[0]

    def kernel(tok_ref, gain_ref, *refs):
        out_ref = refs[-1]
        x = tok_ref[...].astype(f32)
        scale = lax.rsqrt(jnp.mean(x * x, axis=-1, keepdims=True) + eps)
        out_ref[:, :width] = (x * scale * gain_ref[...]).astype(bf16)
        total = jnp.zeros((rows, 128), f32)
        for i in range(4):
            ids = lax.broadcasted_iota(jnp.int32, (top, 128), 0) + i * top
            lanes = lax.broadcasted_iota(jnp.int32, (top, 128), 1)
            move = jnp.where(ids == lanes, 1.0, 0.0).astype(bf16)
            codes = refs[i][...].astype(f32).astype(bf16)
            total = total + lax.dot_general(
                codes, move, (((0,), (0,)), ((), ())), preferred_element_type=f32
            )
        out_ref[:, width:] = total.astype(bf16)

    return pl.pallas_call(
        kernel, out_shape=jax.ShapeDtypeStruct((rows, width + 128), bf16), name="first_rows"
    )(tokens, gain, *tables)


def paired_rows(tokens, gain, cotangent):
    rows, width = tokens.shape

    def kernel(tok_ref, gain_ref, cot_ref, out_ref):
        x = tok_ref[...].astype(f32)
        scale = lax.rsqrt(jnp.mean(x * x, axis=-1, keepdims=True) + eps)
        out_ref[:, :width] = (x * scale * gain_ref[...]).astype(bf16)
        out_ref[:, width:] = cot_ref[...]

    return pl.pallas_call(
        kernel, out_shape=jax.ShapeDtypeStruct((rows, 2 * width), bf16), name="paired_rows"
    )(tokens, gain, cotangent)


def routed_send(blocks, tabled, lane, top, plane, first, width):
    count = len(blocks)
    rows = blocks[0].shape[0]
    slots = most * count
    total = plane * slots
    step = min(1024, width)

    def kernel(first_ref, *refs):
        tab = refs[:count]
        src = refs[count : 2 * count]
        send_ref, place_ref, weigh_ref = refs[2 * count :]

        @pl.when(pl.program_id(0) == 0)
        def _():
            table = jnp.concatenate([r[...] for r in tab], axis=0).astype(f32)
            lanes = lax.broadcasted_iota(jnp.int32, (count * rows, 128), 1)
            wanted = jnp.where(lanes < plane, lanes + first_ref[0], -5).astype(f32)
            named = jnp.zeros((count * rows, 128), f32)
            gates = jnp.zeros((count * rows, 128), f32)
            for k in range(top):
                same = table[:, lane + k : lane + k + 1] == wanted
                named = named + jnp.where(same, 1.0, 0.0)
                gates = gates + jnp.where(same, table[:, lane + top + k : lane + top + k + 1], 0.0)
            r0 = lax.broadcasted_iota(jnp.int32, (rows, rows), 0)
            r1 = lax.broadcasted_iota(jnp.int32, (rows, rows), 1)
            earlier = jnp.where(r1 < r0, 1.0, 0.0).astype(bf16)
            ranks = [
                jnp.dot(
                    earlier,
                    named[j * rows : (j + 1) * rows].astype(bf16),
                    preferred_element_type=f32,
                )
                + float(j * most)
                for j in range(count)
            ]
            code = jnp.where(named > 0.5, jnp.concatenate(ranks, axis=0), -1.0)
            flipped = code.T
            ids = lax.broadcasted_iota(jnp.int32, (slots, count * rows), 0).astype(f32)
            placed = [
                jnp.where(flipped[p : p + 1, :] == ids, 1.0, 0.0) for p in range(plane)
            ]
            place_ref[...] = jnp.concatenate(placed, axis=0).astype(bf16)
            p0 = lax.broadcasted_iota(jnp.int32, (128, total), 0) * slots
            n0 = lax.broadcasted_iota(jnp.int32, (128, total), 1)
            spread = jnp.where((n0 >= p0) & (n0 < p0 + slots), 1.0, 0.0).astype(bf16)
            n1 = lax.broadcasted_iota(jnp.int32, (8, total), 1)
            slot_of = n1
            for p in range(1, plane):
                slot_of = slot_of - jnp.where(n1 >= p * slots, slots, 0)
            slot_of = slot_of.astype(f32)[0:1]
            code = jnp.concatenate([code[j * rows : (j + 1) * rows] for j in order], axis=0)
            gates = jnp.concatenate([gates[j * rows : (j + 1) * rows] for j in order], axis=0)
            wide_code = jnp.dot(code.astype(bf16), spread, preferred_element_type=f32)
            wide_gate = jnp.dot(
                (gates * (1.0 / 256.0)).astype(bf16), spread, preferred_element_type=f32
            )
            weigh_ref[...] = jnp.where(wide_code == slot_of, wide_gate, 0.0).astype(bf16)

        gathered = jnp.concatenate([r[...] for r in src], axis=0)
        send_ref[...] = jnp.dot(
            place_ref[...], gathered, preferred_element_type=f32
        ).astype(bf16)

    at = tabled[0].shape[1] // 128 - 1
    return pl.pallas_call(
        kernel,
        grid=(width // step,),
        in_specs=[pl.BlockSpec(memory_space=pltpu.SMEM)]
        + [pl.BlockSpec((rows, 128), lambda c: (0, at))] * count
        + [pl.BlockSpec((rows, step), lambda c: (0, c))] * count,
        out_specs=[
            pl.BlockSpec((total, step), lambda c: (0, c)),
            pl.BlockSpec((total, count * rows), lambda c: (0, 0)),
            pl.BlockSpec((count * rows, total), lambda c: (0, 0)),
        ],
        out_shape=[
            jax.ShapeDtypeStruct((total, width), bf16),
            jax.ShapeDtypeStruct((total, count * rows), bf16),
            jax.ShapeDtypeStruct((count * rows, total), bf16),
        ],
        name="routed_send",
    )(first, *tabled, *blocks)


def placed_send(blocks, place, width):
    count = len(blocks)
    rows = blocks[0].shape[0]
    total = place.shape[0]
    skip = (blocks[0].shape[1] - width) // min(1024, width)
    step = min(1024, width)

    def kernel(place_ref, *refs):
        gathered = jnp.concatenate([r[...] for r in refs[:count]], axis=0)
        refs[count][...] = jnp.dot(
            place_ref[...], gathered, preferred_element_type=f32
        ).astype(bf16)

    return pl.pallas_call(
        kernel,
        grid=(width // step,),
        in_specs=[pl.BlockSpec((total, count * rows), lambda c: (0, 0))]
        + [pl.BlockSpec((rows, step), lambda c: (0, c + skip))] * count,
        out_specs=pl.BlockSpec((total, step), lambda c: (0, c)),
        out_shape=jax.ShapeDtypeStruct((total, width), bf16),
        name="placed_send",
    )(place, *blocks)


def expert_forward(in_rows, w_first, w_second):
    gate_up = jnp.dot(in_rows, w_first, preferred_element_type=f32)
    hidden_width = w_second.shape[0]
    hidden = (jax.nn.silu(gate_up[:, :hidden_width]) * gate_up[:, hidden_width:]).astype(bf16)
    return jnp.dot(hidden, w_second, preferred_element_type=f32).astype(bf16)


def expert_backward(in_rows, out_grad, w_first, w_second):
    gate_up = jnp.dot(in_rows, w_first, preferred_element_type=f32)
    hidden_width = w_second.shape[0]
    gate_part = gate_up[:, :hidden_width]
    up_part = gate_up[:, hidden_width:]
    sigmoid_gate = jax.nn.sigmoid(gate_part)
    activated = gate_part * sigmoid_gate
    slope = sigmoid_gate * (1.0 + gate_part * (1.0 - sigmoid_gate))
    hidden_grad = lax.dot_general(
        out_grad, w_second, (((1,), (1,)), ((), ())), preferred_element_type=f32
    )
    pre_grad = jnp.concatenate(
        [hidden_grad * up_part * slope, hidden_grad * activated], axis=1
    ).astype(bf16)
    return lax.dot_general(
        pre_grad, w_first, (((1,), (1,)), ((), ())), preferred_element_type=f32
    ).astype(bf16)


def inner(
    fwd_tokens,
    fwd_routes,
    fwd_gates,
    bwd_tokens,
    bwd_routes,
    bwd_gates,
    bwd_cotangent,
    norm_gain,
    weight_in,
    weight_out,
):
    plane = lax.axis_size("x") * lax.axis_size("y")
    _, top = fwd_routes.shape
    width = fwd_tokens.shape[1]
    w_first = weight_in[0, 0]
    w_second = weight_out[0, 0]
    first = (lax.axis_index("z") * plane).astype(jnp.int32).reshape(1)
    tables = tuple(t.T for t in (fwd_routes, fwd_gates, bwd_routes, bwd_gates))
    fwd_blocks = gather_ring(first_rows(fwd_tokens, norm_gain, tables), "z")
    bwd_blocks = gather_ring(paired_rows(bwd_tokens, norm_gain, bwd_cotangent), "z")

    fwd_send, _, fwd_weigh = routed_send(
        fwd_blocks, fwd_blocks, 0, top, plane, first, width
    )
    fwd_rows = plane_exchange(fwd_send, ("x", "y"), plane)
    bwd_send, bwd_place, bwd_weigh = routed_send(
        bwd_blocks, fwd_blocks, 2 * top, top, plane, first, width
    )
    bwd_rows = plane_exchange(bwd_send, ("x", "y"), plane)
    grad_send = placed_send(bwd_blocks, bwd_place, width)
    grad_rows = plane_exchange(grad_send, ("x", "y"), plane)

    fwd_result = expert_forward(fwd_rows, w_first, w_second)
    fwd_back = plane_exchange(fwd_result, ("x", "y"), plane)
    bwd_result = expert_backward(bwd_rows, grad_rows, w_first, w_second)
    bwd_back = plane_exchange(bwd_result, ("x", "y"), plane)

    fwd_moe = reduce_hops(fwd_weigh, fwd_back)
    layer_out = (fwd_tokens.astype(f32) + fwd_moe).astype(bf16)
    passed_forward = shifted(layer_out, "segment", 1)
    norm_grad = reduce_hops(bwd_weigh, bwd_back)
    bwd32 = bwd_tokens.astype(f32)
    bwd_scale = rms_scale(bwd32)
    bwd_base = bwd32 * bwd_scale
    scaled = norm_grad * norm_gain[0]
    input_grad = bwd_cotangent.astype(f32) + bwd_scale * (
        scaled - bwd_base * jnp.mean(scaled * bwd_base, axis=-1, keepdims=True)
    )
    passed_backward = shifted(input_grad.astype(bf16), "segment", -1)
    return (passed_forward, passed_backward)


def solution(mesh):
    cut = Mesh(mesh.devices.reshape(4, 8, 4, 2), ("segment", "z", "x", "y"))
    rows = P(("segment", "z", "x", "y"), None)
    placed = (rows,) * 7 + (
        P("segment", None),
        P("segment", ("z", "x", "y"), None, None),
        P("segment", ("z", "x", "y"), None, None),
    )
    return jax.shard_map(inner, mesh=cut, in_specs=placed, out_specs=(rows, rows), check_vma=False)
```
